32 devices in a mesh: dp: 8 (over z, x), expert: 4 (over y, core).
Axes of the slice: x: 2, y: 2, z: 4, core: 2. Of those that a mesh axis runs over, the one named last changes fastest.
Arguments:
- tokens: bfloat16 [8192, 768], P(('dp', 'expert')), may hold values from -6 to 6
- expert_ids: int32 [8192, 2], P(('dp', 'expert')), may hold values from 0 to 15, all different within a row; in each aligned block of 256 rows (0 to 255, 256 to 511, ...) at most 64 rows name the same one
- gate_fixed: int32 [8192, 2], P(('dp', 'expert')), may hold values from 8192 to 65535
- cotangent: bfloat16 [8192, 768], P(('dp', 'expert')), may hold values from -6 to 6
- w_gate: bfloat16 [16, 768, 384], P('expert'), may hold values from -0.21875 to 0.21875
- w_up: bfloat16 [16, 768, 384], P('expert'), may hold values from -0.21875 to 0.21875
- w_down: bfloat16 [16, 768, 384], P('expert'), may hold values from -0.3125 to 0.3125
Outputs:
- layer_out: bfloat16 [8192, 768], P(('dp', 'expert'))
- input_grad: bfloat16 [8192, 768], P(('dp', 'expert'))
- grad_gate: float32 [16, 768, 384], P('expert', 'dp')
- grad_up: float32 [16, 768, 384], P('expert', 'dp')
- grad_down: float32 [16, 768, 384], P('expert', 'dp')
The draws below stay inside these ranges and needn't reach their ends.
Inputs may be any that keep to these rules, and one draw needn't show every extreme that they name: `expert_ids`: A row names 2 different experts. In each aligned block of 256 rows (the rows of one device) no expert is named by more than 64 rows, and in some block one expert is named by exactly 64 rows.
All inputs are finite; a program needn't handle non-finite values.
Results may differ from the reference program's by a relative error of at most 0.015.
Values may be sent and summed in bfloat16 or wider, within the bound.
A program may use at most 64 MiB of HBM per device.

```python
import math
import jax
import jax.numpy as jnp
import numpy as np
from jax import lax

D = 768
FF = 384
TOP = 2
TOK_DEV = 256
EXPERTS = 16
TOKENS = 8192
CAP = 64
LOAD = 1024


def plant(result, stream_key, low, largest):
    index_at = [jax.random.randint(jax.random.fold_in(stream_key, axis), (), 0, length) for axis, length in enumerate(result.shape)]
    widest = result.shape.index(max(result.shape))
    neighbour = index_at[:widest] + [(index_at[widest] + 1) % result.shape[widest]] + index_at[widest + 1:]
    return result.at[tuple(index_at)].set(low).at[tuple(neighbour)].set(largest)


def raised(drawn, stream_key, source, target, parts, factor):
    owner, partner = [(jnp.arange(drawn.shape[dim]) // (drawn.shape[dim] // parts)).reshape([-1 if axis == dim else 1 for axis in range(drawn.ndim)]) for dim in (source, target)]
    chosen = jax.random.permutation(stream_key, parts)[partner]
    strong = (owner == chosen) | (owner == (partner + parts // 2) % parts)
    return jnp.where(strong, factor * drawn, drawn)


def shard_levels(rng, shape, split, least, top_value):
    loudness, own = 1.0, jax.random.fold_in(rng, 6)
    for dim, shards_of in split:
        steps = jnp.exp(jax.random.uniform(jax.random.fold_in(own, dim), (shards_of,), jnp.float32, least / len(split), top_value / len(split)))
        loudness = loudness * jnp.repeat(steps, shape[dim] // shards_of).reshape([-1 if axis == dim else 1 for axis in range(len(shape))])
    return loudness


def routed_block(key, own, number, rows, amount, top, most, skew):
    ranking = jax.random.permutation(key, amount)
    packed, ordinary = load_shares(amount, rows * top, most, skew, True), load_shares(amount, rows * top, most, skew, False)
    places = jnp.arange(amount)

    def named(lengths, rotation):
        used = int((lengths > 0).sum())
        fixed = max(1, used // 4)
        moved = fixed + (places - fixed + rotation * (used - fixed)) % max(1, amount - fixed)
        return jnp.zeros((amount,), jnp.int32).at[ranking[jnp.where(places < fixed, places, moved)]].set(jnp.asarray(lengths, jnp.int32))

    lengths = jnp.where(number % 4 == 0, named(packed, number // 4), named(ordinary, number - number // 4 - 1))
    mixed = jax.random.permutation(jax.random.fold_in(own, 3), amount)
    donor, receiver = mixed[0:amount // 2 * 2:2], mixed[1:amount // 2 * 2:2]
    margin = jnp.minimum(lengths[donor] - 1, most - lengths[receiver]) // 2
    margin = jnp.where((donor == ranking[0]) | (receiver == ranking[0]) | (lengths[receiver] == 0), 0, jnp.maximum(margin, 0))
    moved = jax.random.randint(jax.random.fold_in(own, 4), (amount // 2,), 0, 1 << 20) % (margin + 1)
    lengths = lengths.at[donor].add(-moved).at[receiver].add(moved)
    items = jnp.searchsorted(jnp.cumsum(lengths), jnp.arange(rows * top), side="right").astype(jnp.int32)
    table = items.reshape(top, rows).T
    table = table[jax.random.permutation(jax.random.fold_in(own, 1), rows)]
    rotation = jax.random.randint(jax.random.fold_in(own, 2), (rows, 1), 0, top)
    return jnp.take_along_axis(table, (jnp.arange(top)[None, :] + rotation) % top, axis=1)


def load_shares(count, total, most, skew, full):
    weights = [(1 << 20) // math.isqrt(standing ** skew) + 1 for standing in range(1, count + 1)]
    largest = most if full else min(most, max(-(-total // count), total * weights[0] // sum(weights)))
    least = 1 if total - largest >= count - 1 else 0
    holding, spare = [largest] + [least] * (count - 1), total - largest - least * (count - 1)
    while spare > 0:
        movable = [i for i in range(1, count) if holding[i] < largest] or [i for i in range(1, count) if holding[i] < most]
        whole, budget = sum([weights[i] for i in movable]), spare
        for i in movable:
            more = min(most - holding[i], max(1, budget * weights[i] // whole), spare)
            holding[i] = holding[i] + more
            spare = spare - more
    return np.array(holding)


def bell_draw(rng, shape, width, most, pieces=(), kind=jnp.bfloat16):
    gain = shard_levels(rng, shape, pieces, -0.22, 0.18) if pieces else 1.0
    drawn = jax.random.normal(rng, shape, jnp.float32) * width * gain
    return jnp.minimum(jnp.maximum(drawn, -most), most).astype(kind)


def noise_with(rng, dims, scale, bound, pieces, heavy, kind=jnp.bfloat16):
    values = scale * jax.random.normal(rng, dims, jnp.float32)
    if pieces:
        values = values * shard_levels(rng, dims, pieces, -0.22, 0.18)
    return jnp.clip(raised(values, jax.random.fold_in(rng, 3), *heavy), -bound, bound).astype(kind)


def setup_inputs(seed: int = 0) -> dict:
    key_list = jax.random.split(jax.random.key(seed), 8)
    tokens = noise_with(key_list[0], (TOKENS, D), 1.0, 6.0, ((0, 32),), (0, 1, 32, 2.75))
    expert_ids_keys = jax.random.split(jax.random.fold_in(key_list[1], 1), TOKENS // TOK_DEV)
    expert_ids_turns = jax.random.permutation(jax.random.fold_in(key_list[1], 3), TOKENS // TOK_DEV)
    expert_ids = jax.vmap(lambda own, number: routed_block(jax.random.fold_in(key_list[1], 2), own, number, TOK_DEV, EXPERTS, TOP, CAP, 1))(expert_ids_keys, expert_ids_turns).reshape((TOKENS, TOP))
    gate_fixed = plant(jax.random.randint(key_list[2], (TOKENS, TOP), 8192, 65536), jax.random.fold_in(key_list[2], 1), 8192, 65535).astype(jnp.int32)
    cotangent = noise_with(key_list[3], (TOKENS, D), 1.0, 6.0, ((0, 32),), (0, 1, 32, 2.75))
    w_gate = bell_draw(key_list[4], (EXPERTS, D, FF), D ** -0.5, 0.21875, ((0, 4),))
    w_up = bell_draw(key_list[5], (EXPERTS, D, FF), D ** -0.5, 0.21875, ((0, 4),))
    w_down = bell_draw(key_list[6], (EXPERTS, D, FF), FF ** -0.5, 0.3125, ((0, 4),))
    return {"tokens": tokens, "expert_ids": expert_ids, "gate_fixed": gate_fixed, "cotangent": cotangent, "w_gate": w_gate, "w_up": w_up, "w_down": w_down}


def matmul(left, right):
    return jnp.dot(left.astype(jnp.float32), right.astype(jnp.float32), precision=lax.Precision.HIGHEST)

def reference(tokens, expert_ids, gate_fixed, cotangent, w_gate, w_up, w_down):
    entries = TOKENS * TOP
    flat_ids = expert_ids.reshape(-1).astype(jnp.int32)
    blocks = flat_ids.reshape(-1, TOK_DEV * TOP)
    onehot = (blocks[:, :, None] == jnp.arange(EXPERTS, dtype=jnp.int32)[None, None, :]).astype(jnp.int32)
    slot_rank = lax.optimization_barrier(jnp.sum((jnp.cumsum(onehot, axis=1) - 1) * onehot, axis=2)).reshape(-1)
    block_of = jnp.arange(entries, dtype=jnp.int32) // (TOK_DEV * TOP)
    position = (block_of * CAP + slot_rank).astype(jnp.int32)
    rows_all = TOKENS // TOK_DEV * CAP
    slot_table = jnp.full((EXPERTS, rows_all), entries, jnp.int32)
    slot_table = slot_table.at[flat_ids, position].set(jnp.arange(entries, dtype=jnp.int32))
    gate_values = jnp.concatenate([gate_fixed.reshape(-1).astype(jnp.float32) / 65536.0, jnp.zeros((1,), jnp.float32)])
    grad_scale = 1.0 / math.sqrt(LOAD)

    def one_expert(totals, inputs):
        out_sum, grad_sum = totals
        rows, gate_w, up_w, down_w = inputs
        is_valid = rows < entries
        token_of = jnp.where(is_valid, rows // TOP, 0).astype(jnp.int32)
        rows_in = jnp.where(is_valid[:, None], tokens[token_of], jnp.zeros((), tokens.dtype))
        slot_gate = gate_values[rows]
        grads_in = (slot_gate[:, None] * cotangent[token_of].astype(jnp.float32)).astype(jnp.bfloat16)
        pre_gate = matmul(rows_in, gate_w)
        pre_up = matmul(rows_in, up_w)
        sigmoid_gate = jax.nn.sigmoid(pre_gate)
        activated = pre_gate * sigmoid_gate
        hidden = (activated * pre_up).astype(jnp.bfloat16)
        outputs = matmul(hidden, down_w.T).astype(jnp.bfloat16)
        hidden_grad = matmul(grads_in, down_w)
        gate_grad = (hidden_grad * pre_up * sigmoid_gate * (1.0 + pre_gate * (1.0 - sigmoid_gate))).astype(jnp.bfloat16)
        up_grad = (hidden_grad * activated).astype(jnp.bfloat16)
        entry_grad = (matmul(gate_grad, gate_w.T) + matmul(up_grad, up_w.T)).astype(jnp.bfloat16)
        out_sum = out_sum.at[token_of].add(slot_gate[:, None] * outputs.astype(jnp.float32))
        grad_sum = grad_sum.at[token_of].add(jnp.where(is_valid[:, None], entry_grad.astype(jnp.float32), jnp.zeros((), jnp.float32)))
        weight_gate = matmul(rows_in.T, gate_grad) * grad_scale
        weight_up = matmul(rows_in.T, up_grad) * grad_scale
        weight_down = matmul(grads_in.T, hidden) * grad_scale
        return ((out_sum, grad_sum), (weight_gate, weight_up, weight_down))
    start = (jnp.zeros((TOKENS, D), jnp.float32), jnp.zeros((TOKENS, D), jnp.float32))
    (out_sum, grad_sum), (grad_gate, grad_up, grad_down) = lax.scan(one_expert, start, (slot_table, w_gate, w_up, w_down))
    return (out_sum.astype(jnp.bfloat16), grad_sum.astype(jnp.bfloat16), grad_gate, grad_up, grad_down)
```

```python
import functools

import jax
import jax.numpy as jnp
from jax import lax
from jax.experimental import pallas as pl
from jax.experimental.pallas import tpu as pltpu
from jax.sharding import PartitionSpec as P

BF = jnp.bfloat16
F32 = jnp.float32


def dot(a, b, ca=1, cb=0):
    return lax.dot_general(a, b, (((ca,), (cb,)), ((), ())), preferred_element_type=F32)


def flipped(me, k):
    out, bit = me, 1
    while bit <= k:
        if k & bit:
            out = out + bit * (1 - 2 * lax.rem(lax.div(me, bit), 2))
        bit *= 2
    return out


def kernel(
    n, inner, outer, top, scale,
    meta, tok, cot, wg_h, wu_h, wd_h,
    out_o, din_o, gg_o, gu_o, gd_o,
    w, meta_r, tok_r, cot_r, hot, slot_gate, xs, gs, ys, ds, y_t, y_r, g_all, x_r, z_s, z_r,
    w_sem, ms_sem, mr_sem, ts_sem, tr_sem, cs_sem, cr_sem, ys_sem, yr_sem, xs_sem, xr_sem, zs_sem, zr_sem,
):
    me = lax.axis_index("expert")
    my_dp = lax.axis_index("dp")
    my_z = lax.div(my_dp, inner)
    my_x = lax.rem(my_dp, inner)
    local, d_model, ff = w.shape[1:]
    tokens = tok.shape[0]
    cap = slot_gate.shape[2]
    rows = g_all.shape[4]
    other_x = 1 - my_x
    partner_dp = my_z * inner + other_x

    def z_peer(k):
        return lax.rem(my_z + k, outer) * inner + my_x

    loads = [pltpu.make_async_copy(h, w.at[i], w_sem.at[i]) for i, h in enumerate((wg_h, wu_h, wd_h))]

    barrier = pltpu.get_barrier_semaphore()
    for k in range(1, n):
        pl.semaphore_signal(barrier, inc=1, device_id={"expert": flipped(me, k)})
    pl.semaphore_signal(barrier, inc=1, device_id={"dp": partner_dp})
    for k in range(1, outer):
        pl.semaphore_signal(barrier, inc=1, device_id={"dp": z_peer(k)})
    pl.semaphore_wait(barrier, (n - 1) + 1 + (outer - 1))

    def send(src, dst, s, r, **where):
        return pltpu.make_async_remote_copy(src_ref=src, dst_ref=dst, send_sem=s, recv_sem=r, device_id=where)

    def meta_copy(k):
        return send(meta, meta_r.at[k], ms_sem.at[k], mr_sem.at[k], expert=flipped(me, k))

    def rows_copy(own, landed, s, r, k):
        if k % 2 == 0 or k == 1:
            return send(own, landed.at[k], s.at[k], r.at[k], expert=flipped(me, k))
        return send(landed.at[k - 1], landed.at[k], s.at[k], r.at[k], expert=flipped(me, 1))

    def tok_copy(k):
        return rows_copy(tok, tok_r, ts_sem, tr_sem, k)

    def cot_copy(k):
        return rows_copy(cot, cot_r, cs_sem, cr_sem, k)

    for k in range(1, n):
        meta_copy(k).start()
    direct = [k for k in range(2, n, 2)] + [1]
    for k in direct:
        tok_copy(k).start()
    for k in direct:
        cot_copy(k).start()
    for c in loads:
        c.start()

    above = (
        lax.broadcasted_iota(jnp.int32, (tokens, tokens), 0)
        < lax.broadcasted_iota(jnp.int32, (tokens, tokens), 1)
    )
    before = jnp.where(above, 1.0, 0.0).astype(BF)
    padded = -(-local // 8) * 8

    def route(k):
        if k:
            meta_copy(k).wait_recv()
            mv = meta_r[k]
        else:
            mv = meta[...]
        expert = lax.broadcasted_iota(jnp.int32, (padded, tokens), 0) + me * local
        hit = jnp.zeros((padded, tokens), F32)
        gate = jnp.zeros((padded, tokens), F32)
        for c in range(top):
            same = mv[c : c + 1] == expert
            hit = hit + jnp.where(same, 1.0, 0.0)
            gate = gate + jnp.where(same, mv[top + c : top + c + 1].astype(F32) * (1.0 / 65536.0), 0.0)
        rank = dot(hit.astype(BF), before)
        rank = jnp.where(hit > 0.5, rank, -1.0)
        slot = lax.broadcasted_iota(jnp.int32, (cap, tokens), 0).astype(F32)
        for i in range(local):
            picked = jnp.where(slot == rank[i : i + 1], 1.0, 0.0)
            hot[k, i * cap : (i + 1) * cap] = picked.astype(BF)
            value = jnp.sum(picked * gate[i : i + 1], axis=1, keepdims=True)
            slot_gate[k, i] = jnp.broadcast_to(value, (cap, 128))

    def take_tokens(k, block):
        got = dot(hot[k], block).astype(BF)
        for i in range(local):
            xs[i, k * cap : (k + 1) * cap] = got[i * cap : (i + 1) * cap]

    def take_grads(k, block):
        got = dot(hot[k], block)
        for i in range(local):
            gs[i, k * cap : (k + 1) * cap] = (
                slot_gate[k, i][:, :1] * got[i * cap : (i + 1) * cap]
            ).astype(BF)

    def arrive(copy_of, take, landed):
        for k in range(2, n, 2):
            copy_of(k).wait_recv()
            copy_of(k + 1).start()
        for k in range(1, n):
            if k % 2 or k == 1:
                copy_of(k).wait_recv()
            take(k, landed[k])

    for k in range(n):
        route(k)
    take_tokens(0, tok[...])
    take_grads(0, cot[...])
    arrive(tok_copy, take_tokens, tok_r)
    arrive(cot_copy, take_grads, cot_r)
    for c in loads:
        c.wait()

    def x_copy(e, a):
        return send(
            g_all.at[other_x, e, a], x_r.at[e, a], xs_sem.at[e, a], xr_sem.at[e, a], dp=partner_dp
        )

    def put(e, a, value):
        for zz in range(outer):
            for xx in range(inner):
                at = (zz * inner + xx) * rows
                g_all[xx, e, a, zz] = value[at : at + rows].astype(BF)
        x_copy(e, a).start()

    def one_expert(e, carry):
        x, g = xs[e], gs[e]
        pre_gate = dot(x, w[0, e])
        pre_up = dot(x, w[1, e])
        sig = jax.nn.sigmoid(pre_gate)
        act = pre_gate * sig
        hidden = (act * pre_up).astype(BF)
        put(e, 2, dot(g, hidden, 0, 0))
        hidden_grad = dot(g, w[2, e])
        gate_grad = (hidden_grad * pre_up * sig * (1.0 + pre_gate * (1.0 - sig))).astype(BF)
        up_grad = (hidden_grad * act).astype(BF)
        put(e, 0, dot(x, gate_grad, 0, 0))
        put(e, 1, dot(x, up_grad, 0, 0))
        o = dot(hidden, w[2, e], 1, 1).astype(BF).astype(F32)
        back = dot(gate_grad, w[0, e], 1, 1) + dot(up_grad, w[1, e], 1, 1)
        back = back.astype(BF)
        for k in range(n):
            ys[k, e] = (slot_gate[k, e][:, :1] * o[k * cap : (k + 1) * cap]).astype(BF)
            ds[k, e] = back[k * cap : (k + 1) * cap]
        return carry

    lax.fori_loop(0, local, one_expert, 0)

    def y_copy(j, k):
        return send(y_t.at[j, k], y_r.at[j, k], ys_sem.at[j, k], yr_sem.at[j, k], expert=flipped(me, k))

    def spread(j, k):
        src = (ys, ds)[j]
        return dot(hot[k], src[k].reshape(local * cap, d_model), 0, 0)

    for j in range(2):
        for k in range(n - 1, 0, -1):
            y_t[j, k] = spread(j, k).astype(BF)
            y_copy(j, k).start()

    def z_copy(k, e, a):
        return send(
            z_s.at[e, a, lax.rem(my_z + k, outer)],
            z_r.at[outer - k, e, a],
            zs_sem.at[k, e, a],
            zr_sem.at[outer - k, e, a],
            dp=z_peer(k),
        )

    order = (2, 0, 1)

    def x_stage(e, carry):
        for a in order:
            x_copy(e, a).wait_recv()
            z_s[e, a] = (g_all[my_x, e, a].astype(F32) + x_r[e, a].astype(F32)).astype(BF)
            for k in range(1, outer):
                z_copy(k, e, a).start()
        return carry

    def finish(e, carry):
        for a, o_ref in ((2, gd_o), (0, gg_o), (1, gu_o)):
            total = z_s[e, a, my_z].astype(F32)
            for k in range(1, outer):
                z_copy(outer - k, e, a).wait_recv()
                total = total + z_r[k, e, a].astype(F32)
            o_ref[e] = total * scale
        return carry

    lax.fori_loop(0, local - 1, x_stage, 0)
    for j, o_ref in enumerate((out_o, din_o)):
        total = spread(j, 0)
        for k in range(1, n):
            y_copy(j, k).wait_recv()
            total = total + y_r[j, k].astype(F32)
        o_ref[...] = total.astype(BF)
    lax.fori_loop(0, local - 1, finish, 0)
    x_stage(local - 1, 0)
    finish(local - 1, 0)

    for k in range(1, n):
        meta_copy(k).wait_send()
        tok_copy(k).wait_send()
        cot_copy(k).wait_send()
        for j in range(2):
            y_copy(j, k).wait_send()

    def drain(e, carry):
        for a in range(3):
            x_copy(e, a).wait_send()
            for k in range(1, outer):
                z_copy(k, e, a).wait_send()
        return carry

    lax.fori_loop(0, local, drain, 0)


def shards(tokens, expert_ids, gate_fixed, cotangent, w_gate, w_up, w_down):
    n = lax.axis_size("expert")
    replicas = lax.axis_size("dp")
    inner = 2
    outer = replicas // inner
    local, d_model, ff = w_gate.shape
    count, top = expert_ids.shape
    cap = count * top * 2 // (local * n)
    rows = d_model // replicas
    scale = float(count * n * replicas * top // (local * n)) ** (-0.5)
    meta = jnp.concatenate(
        [expert_ids.T, gate_fixed.T, jnp.zeros((8 - 2 * top, count), jnp.int32)], axis=0
    )
    vmem = pl.BlockSpec(memory_space=pltpu.VMEM)
    hbm = pl.BlockSpec(memory_space=pl.ANY)
    dma = pltpu.SemaphoreType.DMA
    block = jax.ShapeDtypeStruct((count, d_model), BF)
    grad = jax.ShapeDtypeStruct((local, rows, ff), F32)
    return pl.pallas_call(
        functools.partial(kernel, n, inner, outer, top, scale),
        out_shape=(block, block, grad, grad, grad),
        in_specs=[vmem] * 3 + [hbm] * 3,
        out_specs=(vmem,) * 5,
        scratch_shapes=[
            pltpu.VMEM((3, local, d_model, ff), BF),
            pltpu.VMEM((n, 8, count), jnp.int32),
            pltpu.VMEM((n, count, d_model), BF),
            pltpu.VMEM((n, count, d_model), BF),
            pltpu.VMEM((n, local * cap, count), BF),
            pltpu.VMEM((n, local, cap, 128), F32),
            pltpu.VMEM((local, n * cap, d_model), BF),
            pltpu.VMEM((local, n * cap, d_model), BF),
            pltpu.VMEM((n, local, cap, d_model), BF),
            pltpu.VMEM((n, local, cap, d_model), BF),
            pltpu.VMEM((2, n, count, d_model), BF),
            pltpu.VMEM((2, n, count, d_model), BF),
            pltpu.VMEM((inner, local, 3, outer, rows, ff), BF),
            pltpu.VMEM((local, 3, outer, rows, ff), BF),
            pltpu.VMEM((local, 3, outer, rows, ff), BF),
            pltpu.VMEM((outer, local, 3, rows, ff), BF),
            dma((3,)),
            dma((n,)), dma((n,)), dma((n,)), dma((n,)), dma((n,)), dma((n,)),
            dma((2, n)), dma((2, n)),
            dma((local, 3)), dma((local, 3)),
            dma((outer, local, 3)), dma((outer, local, 3)),
        ],
        compiler_params=pltpu.CompilerParams(
            collective_id=0, has_side_effects=True, vmem_limit_bytes=60 * 1024 * 1024
        ),
    )(meta, tokens, cotangent, w_gate, w_up, w_down)


def solution(mesh):
    return jax.shard_map(
        shards,
        mesh=mesh,
        in_specs=(P(("dp", "expert"), None),) * 4 + (P("expert", None, None),) * 3,
        out_specs=(P(("dp", "expert"), None),) * 2 + (P("expert", "dp", None),) * 3,
        check_vma=False,
    )
```

```python
import functools

import jax
import jax.numpy as jnp
from jax import lax
from jax.experimental import pallas as pl
from jax.experimental.pallas import tpu as pltpu
from jax.sharding import PartitionSpec as P

BF = jnp.bfloat16
F32 = jnp.float32


def dot(a, b, ca=1, cb=0):
    return lax.dot_general(a, b, (((ca,), (cb,)), ((), ())), preferred_element_type=F32)


def flipped(me, k):
    out, bit = me, 1
    while bit <= k:
        if k & bit:
            out = out + bit * (1 - 2 * lax.rem(lax.div(me, bit), 2))
        bit *= 2
    return out


def bit_of(i, b):
    return lax.rem(lax.div(i, 1 << b), 2)


def kernel(
    n, orders, top,
    meta, tok, cot, wg_h, wu_h, wd_h,
    act_o, grad_o,
    w, meta_r, tok_r, cot_r, hot, slot_gate, xs, gs, hs, pre, ys, ds, y_t, y_r, parts,
    w_sem, ms_sem, mr_sem, ts_sem, tr_sem, cs_sem, cr_sem, ys_sem, yr_sem, rs_sem, rr_sem,
    *halves,
):
    bits = len(orders[0])
    landed_at, summed = halves[:bits], halves[bits:]
    me = lax.axis_index("expert")
    my_dp = lax.axis_index("dp")
    local, d_model, ff = w.shape[1:]
    tokens = tok.shape[0]
    cap = slot_gate.shape[2]
    rows = parts.shape[3]

    loads = [pltpu.make_async_copy(h, w.at[i], w_sem.at[i]) for i, h in enumerate((wg_h, wu_h, wd_h))]

    barrier = pltpu.get_barrier_semaphore()
    for k in range(1, n):
        pl.semaphore_signal(barrier, inc=1, device_id={"expert": flipped(me, k)})
    for b in range(bits):
        pl.semaphore_signal(barrier, inc=1, device_id={"dp": flipped(my_dp, 1 << b)})
    pl.semaphore_wait(barrier, (n - 1) + bits)

    def send(src, dst, s, r, **where):
        return pltpu.make_async_remote_copy(src_ref=src, dst_ref=dst, send_sem=s, recv_sem=r, device_id=where)

    def meta_copy(k):
        return send(meta, meta_r.at[k], ms_sem.at[k], mr_sem.at[k], expert=flipped(me, k))

    def rows_copy(own, landed, s, r, k):
        if k % 2 == 0 or k == 1:
            return send(own, landed.at[k], s.at[k], r.at[k], expert=flipped(me, k))
        return send(landed.at[k - 1], landed.at[k], s.at[k], r.at[k], expert=flipped(me, 1))

    def tok_copy(k):
        return rows_copy(tok, tok_r, ts_sem, tr_sem, k)

    def cot_copy(k):
        return rows_copy(cot, cot_r, cs_sem, cr_sem, k)

    for k in range(1, n):
        meta_copy(k).start()
    direct = [k for k in range(2, n, 2)] + [1]
    for k in direct:
        tok_copy(k).start()
    for k in direct:
        cot_copy(k).start()
    for c in loads:
        c.start()

    above = (
        lax.broadcasted_iota(jnp.int32, (tokens, tokens), 0)
        < lax.broadcasted_iota(jnp.int32, (tokens, tokens), 1)
    )
    before = jnp.where(above, 1.0, 0.0).astype(BF)
    padded = -(-local // 8) * 8

    def route(k):
        if k:
            meta_copy(k).wait_recv()
            mv = meta_r[k]
        else:
            mv = meta[...]
        expert = lax.broadcasted_iota(jnp.int32, (padded, tokens), 0) + me * local
        hit = jnp.zeros((padded, tokens), F32)
        gate = jnp.zeros((padded, tokens), F32)
        for c in range(top):
            same = mv[c : c + 1] == expert
            hit = hit + jnp.where(same, 1.0, 0.0)
            gate = gate + jnp.where(same, mv[top + c : top + c + 1].astype(F32) * (1.0 / 65536.0), 0.0)
        rank = dot(hit.astype(BF), before)
        rank = jnp.where(hit > 0.5, rank, -1.0)
        slot = lax.broadcasted_iota(jnp.int32, (cap, tokens), 0).astype(F32)
        for i in range(local):
            picked = jnp.where(slot == rank[i : i + 1], 1.0, 0.0)
            hot[k, i * cap : (i + 1) * cap] = picked.astype(BF)
            value = jnp.sum(picked * gate[i : i + 1], axis=1, keepdims=True)
            slot_gate[k, i] = jnp.broadcast_to(value, (cap, 128))

    def take_tokens(k, block):
        got = dot(hot[k], block).astype(BF)
        for i in range(local):
            xs[i, k * cap : (k + 1) * cap] = got[i * cap : (i + 1) * cap]

    def take_grads(k, block):
        got = dot(hot[k], block)
        for i in range(local):
            gs[i, k * cap : (k + 1) * cap] = (
                slot_gate[k, i][:, :1] * got[i * cap : (i + 1) * cap]
            ).astype(BF)

    def arrive(copy_of, take, landed):
        for k in range(2, n, 2):
            copy_of(k).wait_recv()
            copy_of(k + 1).start()
        for k in range(1, n):
            if k % 2 or k == 1:
                copy_of(k).wait_recv()
            take(k, landed[k])

    def halve(s, e, a):
        b = orders[a][s]
        held = parts if s == 0 else summed[s - 1]
        half = 1 << (bits - 1 - s)
        return send(
            held.at[e, a, pl.ds((1 - bit_of(my_dp, b)) * half, half)],
            landed_at[s].at[e, a],
            rs_sem.at[s, e, a],
            rr_sem.at[s, e, a],
            dp=flipped(my_dp, 1 << b),
        )

    def put(e, a, value):
        for c in range(1 << bits):
            at = sum(((c >> b) & 1) << (bits - 1 - p) for p, b in enumerate(orders[a]))
            parts[e, a, at] = value[c * rows : (c + 1) * rows].astype(BF)
        halve(0, e, a).start()

    def forward(e, carry):
        x = xs[e]
        pre_gate = dot(x, w[0, e])
        pre_up = dot(x, w[1, e])
        pre[0, e] = pre_gate
        pre[1, e] = pre_up
        hidden = (pre_gate * jax.nn.sigmoid(pre_gate) * pre_up).astype(BF)
        hs[e] = hidden
        o = dot(hidden, w[2, e], 1, 1).astype(BF).astype(F32)
        for k in range(n):
            ys[k, e] = (slot_gate[k, e][:, :1] * o[k * cap : (k + 1) * cap]).astype(BF)
        return carry

    def backward(e, carry):
        x, g = xs[e], gs[e]
        put(e, 2, dot(g, hs[e], 0, 0))
        hidden_grad = dot(g, w[2, e])
        pre_gate, pre_up = pre[0, e], pre[1, e]
        sig = jax.nn.sigmoid(pre_gate)
        up_grad = (hidden_grad * (pre_gate * sig)).astype(BF)
        put(e, 1, dot(x, up_grad, 0, 0))
        gate_grad = (hidden_grad * pre_up * sig * (1.0 + pre_gate * (1.0 - sig))).astype(BF)
        put(e, 0, dot(x, gate_grad, 0, 0))
        back = dot(gate_grad, w[0, e], 1, 1) + dot(up_grad, w[1, e], 1, 1)
        back = back.astype(BF)
        for k in range(n):
            ds[k, e] = back[k * cap : (k + 1) * cap]
        return carry

    for k in range(n):
        route(k)
    take_tokens(0, tok[...])
    take_grads(0, cot[...])
    arrive(tok_copy, take_tokens, tok_r)
    for c in loads:
        c.wait()
    lax.fori_loop(0, local, forward, 0)
    arrive(cot_copy, take_grads, cot_r)
    lax.fori_loop(0, local, backward, 0)

    def y_copy(j, k):
        return send(y_t.at[j, k], y_r.at[j, k], ys_sem.at[j, k], yr_sem.at[j, k], expert=flipped(me, k))

    def spread(j, k):
        src = (ys, ds)[j]
        return dot(hot[k], src[k].reshape(local * cap, d_model), 0, 0)

    for j in range(2):
        for k in range(n - 1, 0, -1):
            y_t[j, k] = spread(j, k).astype(BF)
            y_copy(j, k).start()

    def total_of(s, e, a):
        halve(s, e, a).wait_recv()
        held = parts if s == 0 else summed[s - 1]
        half = 1 << (bits - 1 - s)
        mine = held[e, a, pl.ds(bit_of(my_dp, orders[a][s]) * half, half)]
        return mine.astype(F32) + landed_at[s][e, a].astype(F32)

    def step(s, e, a):
        summed[s][e, a] = total_of(s, e, a).astype(BF)
        halve(s + 1, e, a).start()

    def finish(e, a):
        grad_o[a, e] = total_of(bits - 1, e, a)[0]

    def returned(j):
        total = spread(j, 0)
        for k in range(1, n):
            y_copy(j, k).wait_recv()
            total = total + y_r[j, k].astype(F32)
        act_o[j] = total.astype(BF)

    events = []
    first = [(e, a) for e in range(local) for a in (2, 0)]
    other = [(e, 1) for e in range(local)]
    for i, (e, a) in enumerate(first):
        at = i + 1.0
        for s in range(bits):
            events.append((at, step if s < bits - 1 else finish, s, e, a))
            at = (max(at, float(len(other))) if s == 0 else at) + 0.6 / (1 << s)
    for i, (e, a) in enumerate(other):
        at = i + 1.0
        for s in range(bits):
            events.append((at, step if s < bits - 1 else finish, s, e, a))
            at = (len(first) + 0.5 * (i + 1) if s == 0 else at + 0.5 / (1 << s))
    events += [(0.6 * len(first), returned, 0, 0, 0), (0.85 * len(first), returned, 0, 1, 0)]
    for _, what, s, e, a in sorted(events, key=lambda event: event[0]):
        if what is step:
            step(s, e, a)
        elif what is finish:
            finish(e, a)
        else:
            returned(e)

    for k in range(1, n):
        meta_copy(k).wait_send()
        tok_copy(k).wait_send()
        cot_copy(k).wait_send()
        for j in range(2):
            y_copy(j, k).wait_send()

    def drain(e, carry):
        for a in range(3):
            for s in range(bits):
                halve(s, e, a).wait_send()
        return carry

    lax.fori_loop(0, local, drain, 0)


def write(scale, act, grad, out_o, din_o, gg_o, gu_o, gd_o):
    out_o[...] = act[0]
    din_o[...] = act[1]
    for a, o in enumerate((gg_o, gu_o, gd_o)):
        o[...] = grad[a] * scale


def shards(tokens, expert_ids, gate_fixed, cotangent, w_gate, w_up, w_down):
    n = lax.axis_size("expert")
    replicas = lax.axis_size("dp")
    bits = replicas.bit_length() - 1
    straight = tuple(range(bits))
    swapped = straight[:2][::-1] + straight[2:]
    orders = (straight, swapped, straight)
    local, d_model, ff = w_gate.shape
    count, top = expert_ids.shape
    cap = count * top * 2 // (local * n)
    rows = d_model // replicas
    scale = float(count * n * replicas * top // (local * n)) ** (-0.5)
    meta = jnp.concatenate(
        [expert_ids.T, gate_fixed.T, jnp.zeros((8 - 2 * top, count), jnp.int32)], axis=0
    )
    vmem = pl.BlockSpec(memory_space=pltpu.VMEM)
    hbm = pl.BlockSpec(memory_space=pl.ANY)
    dma = pltpu.SemaphoreType.DMA
    halves = [pltpu.VMEM((local, 3, 1 << (bits - 1 - s), rows, ff), BF) for s in range(bits)]
    act, grad = pl.pallas_call(
        functools.partial(kernel, n, orders, top),
        out_shape=(
            jax.ShapeDtypeStruct((2, count, d_model), BF),
            jax.ShapeDtypeStruct((3, local, rows, ff), F32),
        ),
        in_specs=[vmem] * 3 + [hbm] * 3,
        out_specs=(vmem,) * 2,
        scratch_shapes=[
            pltpu.VMEM((3, local, d_model, ff), BF),
            pltpu.VMEM((n, 8, count), jnp.int32),
            pltpu.VMEM((n, count, d_model), BF),
            pltpu.VMEM((n, count, d_model), BF),
            pltpu.VMEM((n, local * cap, count), BF),
            pltpu.VMEM((n, local, cap, 128), F32),
            pltpu.VMEM((local, n * cap, d_model), BF),
            pltpu.VMEM((local, n * cap, d_model), BF),
            pltpu.VMEM((local, n * cap, ff), BF),
            pltpu.VMEM((2, local, n * cap, ff), F32),
            pltpu.VMEM((n, local, cap, d_model), BF),
            pltpu.VMEM((n, local, cap, d_model), BF),
            pltpu.VMEM((2, n, count, d_model), BF),
            pltpu.VMEM((2, n, count, d_model), BF),
            pltpu.VMEM((local, 3, replicas, rows, ff), BF),
            dma((3,)),
            dma((n,)), dma((n,)), dma((n,)), dma((n,)), dma((n,)), dma((n,)),
            dma((2, n)), dma((2, n)),
            dma((bits, local, 3)), dma((bits, local, 3)),
            *halves, *halves[:-1],
        ],
        compiler_params=pltpu.CompilerParams(
            collective_id=0, has_side_effects=True, vmem_limit_bytes=60 * 1024 * 1024
        ),
    )(meta, tokens, cotangent, w_gate, w_up, w_down)
    step = count // local
    act_block = jax.ShapeDtypeStruct((count, d_model), BF)
    grad_block = jax.ShapeDtypeStruct((local, rows, ff), F32)
    row_spec = pl.BlockSpec((step, d_model), lambda i: (i, 0))
    grad_spec = pl.BlockSpec((1, rows, ff), lambda i: (i, 0, 0))
    return pl.pallas_call(
        functools.partial(write, scale),
        grid=(local,),
        out_shape=(act_block, act_block, grad_block, grad_block, grad_block),
        in_specs=[
            pl.BlockSpec((2, step, d_model), lambda i: (0, i, 0)),
            pl.BlockSpec((3, 1, rows, ff), lambda i: (0, i, 0, 0)),
        ],
        out_specs=(row_spec, row_spec, grad_spec, grad_spec, grad_spec),
    )(act, grad)


def solution(mesh):
    return jax.shard_map(
        shards,
        mesh=mesh,
        in_specs=(P(("dp", "expert"), None),) * 4 + (P("expert", None, None),) * 3,
        out_specs=(P(("dp", "expert"), None),) * 2 + (P("expert", "dp", None),) * 3,
        check_vma=False,
    )
```

```python
import functools

import jax
import jax.numpy as jnp
from jax import lax
from jax.experimental import pallas as pl
from jax.experimental.pallas import tpu as pltpu
from jax.sharding import PartitionSpec as P

BF = jnp.bfloat16
F32 = jnp.float32


def dot(a, b, ca=1, cb=0):
    return lax.dot_general(a, b, (((ca,), (cb,)), ((), ())), preferred_element_type=F32)


def flipped(me, k):
    out, bit = me, 1
    while bit <= k:
        if k & bit:
            out = out + bit * (1 - 2 * lax.rem(lax.div(me, bit), 2))
        bit *= 2
    return out


def kernel(
    n, inner, outer, top,
    meta, tok, cot, wg_h, wu_h, wd_h,
    act_o, grad_o,
    w, meta_r, tok_r, cot_r, hot, slot_gate, xs, gs, hs, pre, ys, ds, y_t, y_r, parts,
    w_sem, ms_sem, mr_sem, ts_sem, tr_sem, cs_sem, cr_sem, ys_sem, yr_sem, xs_sem, xr_sem, zs_sem, zr_sem,
    x_r, z_s, z_r,
):
    me = lax.axis_index("expert")
    my_dp = lax.axis_index("dp")
    my_z = lax.div(my_dp, inner)
    my_x = lax.rem(my_dp, inner)
    other_x = 1 - my_x
    partner_dp = my_z * inner + other_x
    local, d_model, ff = w.shape[1:]
    tokens = tok.shape[0]
    cap = slot_gate.shape[2]
    rows = parts.shape[4]

    loads = [pltpu.make_async_copy(h, w.at[i], w_sem.at[i]) for i, h in enumerate((wg_h, wu_h, wd_h))]

    barrier = pltpu.get_barrier_semaphore()
    for k in range(1, n):
        pl.semaphore_signal(barrier, inc=1, device_id={"expert": flipped(me, k)})
    pl.semaphore_signal(barrier, inc=1, device_id={"dp": partner_dp})
    for k in range(1, outer):
        pl.semaphore_signal(barrier, inc=1, device_id={"dp": flipped(my_z, k) * inner + my_x})
    pl.semaphore_wait(barrier, (n - 1) + 1 + (outer - 1))

    def send(src, dst, s, r, **where):
        return pltpu.make_async_remote_copy(src_ref=src, dst_ref=dst, send_sem=s, recv_sem=r, device_id=where)

    def meta_copy(k):
        return send(meta, meta_r.at[k], ms_sem.at[k], mr_sem.at[k], expert=flipped(me, k))

    def rows_copy(own, landed, s, r, k):
        if k % 2 == 0 or k == 1:
            return send(own, landed.at[k], s.at[k], r.at[k], expert=flipped(me, k))
        return send(landed.at[k - 1], landed.at[k], s.at[k], r.at[k], expert=flipped(me, 1))

    def tok_copy(k):
        return rows_copy(tok, tok_r, ts_sem, tr_sem, k)

    def cot_copy(k):
        return rows_copy(cot, cot_r, cs_sem, cr_sem, k)

    for k in range(1, n):
        meta_copy(k).start()
    direct = [k for k in range(2, n, 2)] + [1]
    for k in direct:
        tok_copy(k).start()
    for k in direct:
        cot_copy(k).start()
    for c in loads:
        c.start()

    above = (
        lax.broadcasted_iota(jnp.int32, (tokens, tokens), 0)
        < lax.broadcasted_iota(jnp.int32, (tokens, tokens), 1)
    )
    before = jnp.where(above, 1.0, 0.0).astype(BF)
    padded = -(-local // 8) * 8

    def route(k):
        if k:
            meta_copy(k).wait_recv()
            mv = meta_r[k]
        else:
            mv = meta[...]
        expert = lax.broadcasted_iota(jnp.int32, (padded, tokens), 0) + me * local
        hit = jnp.zeros((padded, tokens), F32)
        gate = jnp.zeros((padded, tokens), F32)
        for c in range(top):
            same = mv[c : c + 1] == expert
            hit = hit + jnp.where(same, 1.0, 0.0)
            gate = gate + jnp.where(same, mv[top + c : top + c + 1].astype(F32) * (1.0 / 65536.0), 0.0)
        rank = dot(hit.astype(BF), before)
        rank = jnp.where(hit > 0.5, rank, -1.0)
        slot = lax.broadcasted_iota(jnp.int32, (cap, tokens), 0).astype(F32)
        for i in range(local):
            picked = jnp.where(slot == rank[i : i + 1], 1.0, 0.0)
            hot[k, i * cap : (i + 1) * cap] = picked.astype(BF)
            value = jnp.sum(picked * gate[i : i + 1], axis=1, keepdims=True)
            slot_gate[k, i] = jnp.broadcast_to(value, (cap, 128))

    def take_tokens(k, block):
        got = dot(hot[k], block).astype(BF)
        for i in range(local):
            xs[i, k * cap : (k + 1) * cap] = got[i * cap : (i + 1) * cap]

    def take_grads(k, block):
        got = dot(hot[k], block)
        for i in range(local):
            gs[i, k * cap : (k + 1) * cap] = (
                slot_gate[k, i][:, :1] * got[i * cap : (i + 1) * cap]
            ).astype(BF)

    def arrive(copy_of, take, landed):
        for k in range(2, n, 2):
            copy_of(k).wait_recv()
            copy_of(k + 1).start()
        for k in range(1, n):
            if k % 2 or k == 1:
                copy_of(k).wait_recv()
            take(k, landed[k])

    def x_copy(e, a):
        return send(
            parts.at[other_x, e, a], x_r.at[e, a], xs_sem.at[e, a], xr_sem.at[e, a], dp=partner_dp
        )

    def z_copy(k, e, a):
        there = flipped(my_z, k)
        return send(
            z_s.at[e, a, there], z_r.at[k, e, a], zs_sem.at[k, e, a], zr_sem.at[k, e, a],
            dp=there * inner + my_x,
        )

    def put(e, a, value):
        for zz in range(outer):
            for xx in range(inner):
                at = (zz * inner + xx) * rows
                parts[xx, e, a, zz] = value[at : at + rows].astype(BF)
        x_copy(e, a).start()

    def forward(e, carry):
        x = xs[e]
        pre_gate = dot(x, w[0, e])
        pre_up = dot(x, w[1, e])
        pre[0, e] = pre_gate
        pre[1, e] = pre_up
        hidden = (pre_gate * jax.nn.sigmoid(pre_gate) * pre_up).astype(BF)
        hs[e] = hidden
        o = dot(hidden, w[2, e], 1, 1).astype(BF).astype(F32)
        for k in range(n):
            ys[k, e] = (slot_gate[k, e][:, :1] * o[k * cap : (k + 1) * cap]).astype(BF)
        return carry

    def backward(e, carry):
        x, g = xs[e], gs[e]
        put(e, 2, dot(g, hs[e], 0, 0))
        hidden_grad = dot(g, w[2, e])
        pre_gate, pre_up = pre[0, e], pre[1, e]
        sig = jax.nn.sigmoid(pre_gate)
        up_grad = (hidden_grad * (pre_gate * sig)).astype(BF)
        put(e, 1, dot(x, up_grad, 0, 0))
        gate_grad = (hidden_grad * pre_up * sig * (1.0 + pre_gate * (1.0 - sig))).astype(BF)
        put(e, 0, dot(x, gate_grad, 0, 0))
        back = dot(gate_grad, w[0, e], 1, 1) + dot(up_grad, w[1, e], 1, 1)
        back = back.astype(BF)
        for k in range(n):
            ds[k, e] = back[k * cap : (k + 1) * cap]
        return carry

    for k in range(n):
        route(k)
    take_tokens(0, tok[...])
    take_grads(0, cot[...])
    arrive(tok_copy, take_tokens, tok_r)
    for c in loads:
        c.wait()
    lax.fori_loop(0, local, forward, 0)
    arrive(cot_copy, take_grads, cot_r)
    lax.fori_loop(0, local, backward, 0)

    def y_copy(j, k):
        return send(y_t.at[j, k], y_r.at[j, k], ys_sem.at[j, k], yr_sem.at[j, k], expert=flipped(me, k))

    def spread(j, k):
        src = (ys, ds)[j]
        return dot(hot[k], src[k].reshape(local * cap, d_model), 0, 0)

    for j in range(2):
        for k in range(n - 1, 0, -1):
            y_t[j, k] = spread(j, k).astype(BF)
            y_copy(j, k).start()

    def x_stage(e, carry):
        for a in (2, 1, 0):
            x_copy(e, a).wait_recv()
            z_s[e, a] = (parts[my_x, e, a].astype(F32) + x_r[e, a].astype(F32)).astype(BF)
            for k in range(outer - 1, 0, -1):
                z_copy(k, e, a).start()
        return carry

    def finish(e, carry):
        for a in (2, 1, 0):
            total = z_s[e, a, my_z].astype(F32)
            for k in range(1, outer):
                z_copy(k, e, a).wait_recv()
                total = total + z_r[k, e, a].astype(F32)
            grad_o[a, e] = total
        return carry

    def returned(j):
        total = spread(j, 0)
        for k in range(1, n):
            y_copy(j, k).wait_recv()
            total = total + y_r[j, k].astype(F32)
        act_o[j] = total.astype(BF)

    lax.fori_loop(0, local - 1, x_stage, 0)
    for j in range(2):
        returned(j)
    lax.fori_loop(0, local - 2, finish, 0)
    x_stage(local - 1, 0)
    finish(local - 2, 0)
    finish(local - 1, 0)

    for k in range(1, n):
        meta_copy(k).wait_send()
        tok_copy(k).wait_send()
        cot_copy(k).wait_send()
        for j in range(2):
            y_copy(j, k).wait_send()

    def drain(e, carry):
        for a in range(3):
            x_copy(e, a).wait_send()
            for k in range(1, outer):
                z_copy(k, e, a).wait_send()
        return carry

    lax.fori_loop(0, local, drain, 0)


def write(scale, act, grad, out_o, din_o, gg_o, gu_o, gd_o):
    out_o[...] = act[0]
    din_o[...] = act[1]
    for a, o in enumerate((gg_o, gu_o, gd_o)):
        o[...] = grad[a] * scale


def shards(tokens, expert_ids, gate_fixed, cotangent, w_gate, w_up, w_down):
    n = lax.axis_size("expert")
    replicas = lax.axis_size("dp")
    inner = 2
    outer = replicas // inner
    local, d_model, ff = w_gate.shape
    count, top = expert_ids.shape
    cap = count * top * 2 // (local * n)
    rows = d_model // replicas
    scale = float(count * n * replicas * top // (local * n)) ** (-0.5)
    meta = jnp.concatenate(
        [expert_ids.T, gate_fixed.T, jnp.zeros((8 - 2 * top, count), jnp.int32)], axis=0
    )
    vmem = pl.BlockSpec(memory_space=pltpu.VMEM)
    hbm = pl.BlockSpec(memory_space=pl.ANY)
    dma = pltpu.SemaphoreType.DMA
    half = pltpu.VMEM((local, 3, outer, rows, ff), BF)
    act, grad = pl.pallas_call(
        functools.partial(kernel, n, inner, outer, top),
        out_shape=(
            jax.ShapeDtypeStruct((2, count, d_model), BF),
            jax.ShapeDtypeStruct((3, local, rows, ff), F32),
        ),
        in_specs=[vmem] * 3 + [hbm] * 3,
        out_specs=(vmem,) * 2,
        scratch_shapes=[
            pltpu.VMEM((3, local, d_model, ff), BF),
            pltpu.VMEM((n, 8, count), jnp.int32),
            pltpu.VMEM((n, count, d_model), BF),
            pltpu.VMEM((n, count, d_model), BF),
            pltpu.VMEM((n, local * cap, count), BF),
            pltpu.VMEM((n, local, cap, 128), F32),
            pltpu.VMEM((local, n * cap, d_model), BF),
            pltpu.VMEM((local, n * cap, d_model), BF),
            pltpu.VMEM((local, n * cap, ff), BF),
            pltpu.VMEM((2, local, n * cap, ff), F32),
            pltpu.VMEM((n, local, cap, d_model), BF),
            pltpu.VMEM((n, local, cap, d_model), BF),
            pltpu.VMEM((2, n, count, d_model), BF),
            pltpu.VMEM((2, n, count, d_model), BF),
            pltpu.VMEM((inner, local, 3, outer, rows, ff), BF),
            dma((3,)),
            dma((n,)), dma((n,)), dma((n,)), dma((n,)), dma((n,)), dma((n,)),
            dma((2, n)), dma((2, n)),
            dma((local, 3)), dma((local, 3)),
            dma((outer, local, 3)), dma((outer, local, 3)),
            half, half, pltpu.VMEM((outer, local, 3, rows, ff), BF),
        ],
        compiler_params=pltpu.CompilerParams(
            collective_id=0, has_side_effects=True, vmem_limit_bytes=60 * 1024 * 1024
        ),
    )(meta, tokens, cotangent, w_gate, w_up, w_down)
    step = count // local
    act_block = jax.ShapeDtypeStruct((count, d_model), BF)
    grad_block = jax.ShapeDtypeStruct((local, rows, ff), F32)
    return pl.pallas_call(
        functools.partial(write, scale),
        out_shape=(act_block, act_block, grad_block, grad_block, grad_block),
        in_specs=[vmem] * 2,
        out_specs=(vmem,) * 5,
    )(act, grad)


def solution(mesh):
    return jax.shard_map(
        shards,
        mesh=mesh,
        in_specs=(P(("dp", "expert"), None),) * 4 + (P("expert", None, None),) * 3,
        out_specs=(P(("dp", "expert"), None),) * 2 + (P("expert", "dp", None),) * 3,
        check_vma=False,
    )
```

```python
import functools

import jax
import jax.numpy as jnp
from jax import lax
from jax.experimental import pallas as pl
from jax.experimental.pallas import tpu as pltpu
from jax.sharding import PartitionSpec as P

BF = jnp.bfloat16
F32 = jnp.float32


def dot(a, b, ca=1, cb=0):
    return lax.dot_general(a, b, (((ca,), (cb,)), ((), ())), preferred_element_type=F32)


def flipped(me, k):
    out, bit = me, 1
    while bit <= k:
        if k & bit:
            out = out + bit * (1 - 2 * lax.rem(lax.div(me, bit), 2))
        bit *= 2
    return out


def kernel(
    n, inner, outer, top,
    meta, tok, cot, wg_h, wu_h, wd_h,
    act_o, grad_o,
    w, meta_r, tok_r, cot_r, hot, slot_gate, xs, gs, hs, pre, ys, ds, y_t, y_r, parts,
    w_sem, ms_sem, mr_sem, ts_sem, tr_sem, cs_sem, cr_sem, ys_sem, yr_sem, xs_sem, xr_sem, zs_sem, zr_sem,
    x_r, z_s, z_r,
):
    me = lax.axis_index("expert")
    my_dp = lax.axis_index("dp")
    my_z = lax.div(my_dp, inner)
    my_x = lax.rem(my_dp, inner)
    other_x = 1 - my_x
    partner_dp = my_z * inner + other_x
    local, d_model, ff = w.shape[1:]
    tokens = tok.shape[0]
    cap = slot_gate.shape[2]
    rows = parts.shape[4]

    loads = [pltpu.make_async_copy(h, w.at[i], w_sem.at[i]) for i, h in enumerate((wg_h, wu_h, wd_h))]

    barrier = pltpu.get_barrier_semaphore()
    for k in range(1, n):
        pl.semaphore_signal(barrier, inc=1, device_id={"expert": flipped(me, k)})
    pl.semaphore_signal(barrier, inc=1, device_id={"dp": partner_dp})
    for k in range(1, outer):
        pl.semaphore_signal(barrier, inc=1, device_id={"dp": flipped(my_z, k) * inner + my_x})
    pl.semaphore_wait(barrier, (n - 1) + 1 + (outer - 1))

    def send(src, dst, s, r, **where):
        return pltpu.make_async_remote_copy(src_ref=src, dst_ref=dst, send_sem=s, recv_sem=r, device_id=where)

    def meta_copy(k):
        return send(meta, meta_r.at[k], ms_sem.at[k], mr_sem.at[k], expert=flipped(me, k))

    def rows_copy(own, landed, s, r, k):
        if k % 2 == 0 or k == 1:
            return send(own, landed.at[k], s.at[k], r.at[k], expert=flipped(me, k))
        return send(landed.at[k - 1], landed.at[k], s.at[k], r.at[k], expert=flipped(me, 1))

    def tok_copy(k):
        return rows_copy(tok, tok_r, ts_sem, tr_sem, k)

    def cot_copy(k):
        return rows_copy(cot, cot_r, cs_sem, cr_sem, k)

    for k in range(1, n):
        meta_copy(k).start()
    direct = [k for k in range(2, n, 2)] + [1]
    for k in direct:
        tok_copy(k).start()
    for k in direct:
        cot_copy(k).start()
    for c in loads:
        c.start()

    above = (
        lax.broadcasted_iota(jnp.int32, (tokens, tokens), 0)
        < lax.broadcasted_iota(jnp.int32, (tokens, tokens), 1)
    )
    before = jnp.where(above, 1.0, 0.0).astype(BF)
    padded = -(-local // 8) * 8

    def route(k):
        if k:
            meta_copy(k).wait_recv()
            mv = meta_r[k]
        else:
            mv = meta[...]
        expert = lax.broadcasted_iota(jnp.int32, (padded, tokens), 0) + me * local
        hit = jnp.zeros((padded, tokens), F32)
        gate = jnp.zeros((padded, tokens), F32)
        for c in range(top):
            same = mv[c : c + 1] == expert
            hit = hit + jnp.where(same, 1.0, 0.0)
            gate = gate + jnp.where(same, mv[top + c : top + c + 1].astype(F32) * (1.0 / 65536.0), 0.0)
        rank = dot(hit.astype(BF), before)
        rank = jnp.where(hit > 0.5, rank, -1.0)
        slot = lax.broadcasted_iota(jnp.int32, (cap, tokens), 0).astype(F32)
        for i in range(local):
            picked = jnp.where(slot == rank[i : i + 1], 1.0, 0.0)
            hot[k, i * cap : (i + 1) * cap] = picked.astype(BF)
            value = jnp.sum(picked * gate[i : i + 1], axis=1, keepdims=True)
            slot_gate[k, i] = jnp.broadcast_to(value, (cap, 128))

    def take_tokens(k, block):
        got = dot(hot[k], block).astype(BF)
        for i in range(local):
            xs[i, k * cap : (k + 1) * cap] = got[i * cap : (i + 1) * cap]

    def take_grads(k, block):
        got = dot(hot[k], block)
        for i in range(local):
            gs[i, k * cap : (k + 1) * cap] = (
                slot_gate[k, i][:, :1] * got[i * cap : (i + 1) * cap]
            ).astype(BF)

    def arrive(copy_of, take, landed):
        for k in range(2, n, 2):
            copy_of(k).wait_recv()
            copy_of(k + 1).start()
        for k in range(1, n):
            if k % 2 or k == 1:
                copy_of(k).wait_recv()
            take(k, landed[k])

    def x_copy(e, a):
        return send(
            parts.at[other_x, e, a], x_r.at[e, a], xs_sem.at[e, a], xr_sem.at[e, a], dp=partner_dp
        )

    def z_copy(k, e, a):
        there = flipped(my_z, k)
        return send(
            z_s.at[e, a, there], z_r.at[k, e, a], zs_sem.at[k, e, a], zr_sem.at[k, e, a],
            dp=there * inner + my_x,
        )

    def put(e, a, value):
        for zz in range(outer):
            for xx in range(inner):
                at = (zz * inner + xx) * rows
                parts[xx, e, a, zz] = value[at : at + rows].astype(BF)
        x_copy(e, a).start()

    def forward(e, carry):
        x = xs[e]
        pre_gate = dot(x, w[0, e])
        pre_up = dot(x, w[1, e])
        pre[0, e] = pre_gate
        pre[1, e] = pre_up
        hidden = (pre_gate * jax.nn.sigmoid(pre_gate) * pre_up).astype(BF)
        hs[e] = hidden
        o = dot(hidden, w[2, e], 1, 1).astype(BF).astype(F32)
        for k in range(n):
            ys[k, e] = (slot_gate[k, e][:, :1] * o[k * cap : (k + 1) * cap]).astype(BF)
        return carry

    def backward(e, carry):
        x, g = xs[e], gs[e]
        put(e, 2, dot(g, hs[e], 0, 0))
        hidden_grad = dot(g, w[2, e])
        pre_gate, pre_up = pre[0, e], pre[1, e]
        sig = jax.nn.sigmoid(pre_gate)
        up_grad = (hidden_grad * (pre_gate * sig)).astype(BF)
        put(e, 1, dot(x, up_grad, 0, 0))
        gate_grad = (hidden_grad * pre_up * sig * (1.0 + pre_gate * (1.0 - sig))).astype(BF)
        put(e, 0, dot(x, gate_grad, 0, 0))
        back = dot(gate_grad, w[0, e], 1, 1) + dot(up_grad, w[1, e], 1, 1)
        back = back.astype(BF)
        for k in range(n):
            ds[k, e] = back[k * cap : (k + 1) * cap]
        return carry

    for k in range(n):
        route(k)
    take_tokens(0, tok[...])
    take_grads(0, cot[...])
    arrive(tok_copy, take_tokens, tok_r)
    for c in loads:
        c.wait()
    lax.fori_loop(0, local, forward, 0)
    arrive(cot_copy, take_grads, cot_r)
    lax.fori_loop(0, local, backward, 0)

    def y_copy(j, k):
        return send(y_t.at[j, k], y_r.at[j, k], ys_sem.at[j, k], yr_sem.at[j, k], expert=flipped(me, k))

    def spread(j, k):
        src = (ys, ds)[j]
        return dot(hot[k], src[k].reshape(local * cap, d_model), 0, 0)

    def x_stage(e, carry):
        for a in (2, 1, 0):
            x_copy(e, a).wait_recv()
            z_s[e, a] = (parts[my_x, e, a].astype(F32) + x_r[e, a].astype(F32)).astype(BF)
            for k in range(1, outer):
                z_copy(k, e, a).start()
        return carry

    def finish(e, carry):
        for a in (2, 1, 0):
            total = z_s[e, a, my_z].astype(F32)
            for k in range(1, outer):
                z_copy(k, e, a).wait_recv()
                total = total + z_r[k, e, a].astype(F32)
            grad_o[a, e] = total
        return carry

    def returned(j):
        total = spread(j, 0)
        for k in range(1, n):
            y_copy(j, k).wait_recv()
            total = total + y_r[j, k].astype(F32)
        act_o[j] = total.astype(BF)

    x_stage(0, 0)
    for j in range(2):
        for k in range(n - 1, 0, -1):
            y_t[j, k] = spread(j, k).astype(BF)
            y_copy(j, k).start()
    lax.fori_loop(1, local - 1, x_stage, 0)
    for j in range(2):
        returned(j)
    lax.fori_loop(0, local - 2, finish, 0)
    x_stage(local - 1, 0)
    finish(local - 2, 0)
    finish(local - 1, 0)

    for k in range(1, n):
        meta_copy(k).wait_send()
        tok_copy(k).wait_send()
        cot_copy(k).wait_send()
        for j in range(2):
            y_copy(j, k).wait_send()

    def drain(e, carry):
        for a in range(3):
            x_copy(e, a).wait_send()
            for k in range(1, outer):
                z_copy(k, e, a).wait_send()
        return carry

    lax.fori_loop(0, local, drain, 0)


def write(scale, act, grad, out_o, din_o, gg_o, gu_o, gd_o):
    out_o[...] = act[0]
    din_o[...] = act[1]
    for a, o in enumerate((gg_o, gu_o, gd_o)):
        o[...] = grad[a] * scale


def shards(tokens, expert_ids, gate_fixed, cotangent, w_gate, w_up, w_down):
    n = lax.axis_size("expert")
    replicas = lax.axis_size("dp")
    inner = 2
    outer = replicas // inner
    local, d_model, ff = w_gate.shape
    count, top = expert_ids.shape
    cap = count * top * 2 // (local * n)
    rows = d_model // replicas
    scale = float(count * n * replicas * top // (local * n)) ** (-0.5)
    meta = jnp.concatenate(
        [expert_ids.T, gate_fixed.T, jnp.zeros((8 - 2 * top, count), jnp.int32)], axis=0
    )
    vmem = pl.BlockSpec(memory_space=pltpu.VMEM)
    hbm = pl.BlockSpec(memory_space=pl.ANY)
    dma = pltpu.SemaphoreType.DMA
    half = pltpu.VMEM((local, 3, outer, rows, ff), BF)
    act, grad = pl.pallas_call(
        functools.partial(kernel, n, inner, outer, top),
        out_shape=(
            jax.ShapeDtypeStruct((2, count, d_model), BF),
            jax.ShapeDtypeStruct((3, local, rows, ff), F32),
        ),
        in_specs=[vmem] * 3 + [hbm] * 3,
        out_specs=(vmem,) * 2,
        scratch_shapes=[
            pltpu.VMEM((3, local, d_model, ff), BF),
            pltpu.VMEM((n, 8, count), jnp.int32),
            pltpu.VMEM((n, count, d_model), BF),
            pltpu.VMEM((n, count, d_model), BF),
            pltpu.VMEM((n, local * cap, count), BF),
            pltpu.VMEM((n, local, cap, 128), F32),
            pltpu.VMEM((local, n * cap, d_model), BF),
            pltpu.VMEM((local, n * cap, d_model), BF),
            pltpu.VMEM((local, n * cap, ff), BF),
            pltpu.VMEM((2, local, n * cap, ff), F32),
            pltpu.VMEM((n, local, cap, d_model), BF),
            pltpu.VMEM((n, local, cap, d_model), BF),
            pltpu.VMEM((2, n, count, d_model), BF),
            pltpu.VMEM((2, n, count, d_model), BF),
            pltpu.VMEM((inner, local, 3, outer, rows, ff), BF),
            dma((3,)),
            dma((n,)), dma((n,)), dma((n,)), dma((n,)), dma((n,)), dma((n,)),
            dma((2, n)), dma((2, n)),
            dma((local, 3)), dma((local, 3)),
            dma((outer, local, 3)), dma((outer, local, 3)),
            half, half, pltpu.VMEM((outer, local, 3, rows, ff), BF),
        ],
        compiler_params=pltpu.CompilerParams(
            collective_id=0, has_side_effects=True, vmem_limit_bytes=60 * 1024 * 1024
        ),
    )(meta, tokens, cotangent, w_gate, w_up, w_down)
    step = count // local
    act_block = jax.ShapeDtypeStruct((count, d_model), BF)
    grad_block = jax.ShapeDtypeStruct((local, rows, ff), F32)
    return pl.pallas_call(
        functools.partial(write, scale),
        out_shape=(act_block, act_block, grad_block, grad_block, grad_block),
        in_specs=[vmem] * 2,
        out_specs=(vmem,) * 5,
    )(act, grad)


def solution(mesh):
    return jax.shard_map(
        shards,
        mesh=mesh,
        in_specs=(P(("dp", "expert"), None),) * 4 + (P("expert", None, None),) * 3,
        out_specs=(P(("dp", "expert"), None),) * 2 + (P("expert", "dp", None),) * 3,
        check_vma=False,
    )
```
